256 devices in a mesh: obs: 8 (over z_hi, core), horiz: 32 (over y, z_lo, x).
Axes of the slice: x: 4, y: 4, z: 8 (z_hi: 4, z_lo: 2; z = z_hi * 2 + z_lo), core: 2. Of those that a mesh axis runs over, the one named last changes fastest.
Arguments:
- control: float32 [128, 64, 4096], P(None, 'obs', 'horiz'), may hold values from -6 to 6
- spread: float32 [128, 64, 4096], P(None, 'obs', 'horiz'), may hold values from 0.3 to 3
- vert_root: float32 [128, 128], replicated, as said below
- wind_lon: float32 [128, 64, 4096], P('horiz', 'obs'), may hold values from -0.45 to 0.45
- wind_lat: float32 [128, 64, 4096], P('horiz', 'obs'), may hold values from -0.45 to 0.45
- obs_dest: int32 [262144, 1], P(('obs', 'horiz')), may hold values from 0 to 31; in each aligned block of 1024 rows (0 to 1023, 1024 to 2047, ...) at most 64 rows name the same one
- obs_cells: int32 [4, 262144], P(None, ('obs', 'horiz')), may hold values from 0 to 131071
- obs_time: int32 [262144], P(('obs', 'horiz')), may hold values from 0 to 4
- obs_value: float32 [262144], P(('obs', 'horiz')), may hold values from -6 to 6
- obs_weight: float32 [4, 262144], P(None, ('obs', 'horiz')), may hold values from 0 to 1
- obs_rinv: float32 [262144], P(('obs', 'horiz')), may hold values from 0.3 to 3
Outputs:
- gradient: float32 [128, 64, 4096], P(None, 'obs', 'horiz')
- departure: float32 [262144], P(('obs', 'horiz'))
The draws below stay inside these ranges and needn't reach their ends.
Inputs may be any that keep to these rules, and one draw needn't show every extreme that they name: `obs_dest`: in the rows of one device at most 64 observations name the same level group, a bound that some block reaches. `obs_cells`: cell index within the owner's block of 128 / 32 levels, 8 rows and 4096 longitudes, flattened in that order. `vert_root`: zero beyond 12 places from the diagonal; diagonal entries from 1 to 1.5.
All inputs are finite; a program needn't handle non-finite values.
Results may differ from the reference program's by a relative error of at most 0.00012.
Values sent between devices are 32-bit elements; how exact they have to be, the bound alone decides.
A program may use at most 64 MiB of HBM per device.

```python
import math
import jax
import jax.numpy as jnp
import numpy as np
from jax import lax

LEV = 128
CLAT = 8
NLON = 4096
NT = 4
VBAND = 12
NOBS_DEV = 1024
CAP = 64
NLAT = 64
NOBS = 262144
N_HORIZ = 32


def draw_vert_root(key, part):
    first_key, second_key = jax.random.split(jax.random.fold_in(key, 17))
    row_index = jnp.arange(LEV)[:, None]
    col_index = jnp.arange(LEV)[None, :]
    off_band = jax.random.uniform(first_key, (LEV, LEV), jnp.float32, -0.3, 0.3)
    diagonal = jax.random.uniform(second_key, (LEV, LEV), jnp.float32, 1.0, 1.5)
    inside = jnp.abs(row_index - col_index) <= VBAND
    return jnp.where(row_index == col_index, diagonal, jnp.where(inside, off_band, 0.0)).astype(jnp.float32)


def place_ends(values, rng, smallest, high):
    dims = values.shape
    place = [jax.random.randint(jax.random.fold_in(rng, axis), (), 0, dims[axis]) for axis in range(len(dims))]
    values = values.at[tuple(place)].set(smallest)
    longest = dims.index(max(dims))
    place[longest] = (place[longest] + 1) % dims[longest]
    return values.at[tuple(place)].set(high)


def block_scale(stream_key, shape, cuts, least, top_value):
    def one(dim, parts):
        heights = jax.random.uniform(jax.random.fold_in(jax.random.fold_in(stream_key, 6), dim), (parts,), jnp.float32, least / len(cuts), top_value / len(cuts))
        return jnp.repeat(jnp.exp(heights), shape[dim] // parts).reshape((-1,) + (1,) * (len(shape) - dim - 1))

    loudness = one(*cuts[0])
    for cut in cuts[1:]:
        loudness = loudness * one(*cut)
    return loudness


def assign_block(rng, own, number, rows, amount, top, limit, slope):
    ranking = jax.random.permutation(rng, amount)
    crowded, usual = portions_of(amount, rows * top, limit, slope, True), portions_of(amount, rows * top, limit, slope, False)
    places = jnp.arange(amount)

    def named(tallies, rotation):
        used = int((tallies > 0).sum())
        fixed = max(1, used // 4)
        shifted = fixed + (places - fixed + rotation * (used - fixed)) % max(1, amount - fixed)
        return jnp.zeros((amount,), jnp.int32).at[ranking[jnp.where(places < fixed, places, shifted)]].set(jnp.asarray(tallies, jnp.int32))

    tallies = jnp.where(number % 4 == 0, named(crowded, number // 4), named(usual, number - number // 4 - 1))
    mixed = jax.random.permutation(jax.random.fold_in(own, 3), amount)
    donor, receiver = mixed[0:amount // 2 * 2:2], mixed[1:amount // 2 * 2:2]
    margin = jnp.minimum(tallies[donor] - 1, limit - tallies[receiver]) // 2
    margin = jnp.where((donor == ranking[0]) | (receiver == ranking[0]) | (tallies[receiver] == 0), 0, jnp.maximum(margin, 0))
    shifted = jax.random.randint(jax.random.fold_in(own, 4), (amount // 2,), 0, 1 << 20) % (margin + 1)
    tallies = tallies.at[donor].add(-shifted).at[receiver].add(shifted)
    items = jnp.searchsorted(jnp.cumsum(tallies), jnp.arange(rows * top), side="right").astype(jnp.int32)
    grid = items.reshape(top, rows).T
    grid = grid[jax.random.permutation(jax.random.fold_in(own, 1), rows)]
    rotation = jax.random.randint(jax.random.fold_in(own, 2), (rows, 1), 0, top)
    return jnp.take_along_axis(grid, (jnp.arange(top)[None, :] + rotation) % top, axis=1)


def portions_of(number_of, total, most, lean, full):
    portions = [(1 << 20) // math.isqrt(rank ** lean) + 1 for rank in range(1, number_of + 1)]
    largest = most if full else min(most, max(-(-total // number_of), total * portions[0] // sum(portions)))
    least = 1 if total - largest >= number_of - 1 else 0
    holding, spare = [largest] + [least] * (number_of - 1), total - largest - least * (number_of - 1)
    while spare > 0:
        movable = [i for i in range(1, number_of) if holding[i] < largest] or [i for i in range(1, number_of) if holding[i] < most]
        whole, remaining = sum([portions[i] for i in movable]), spare
        for i in movable:
            extra = min(most - holding[i], max(1, remaining * portions[i] // whole), spare)
            holding[i] = holding[i] + extra
            spare = spare - extra
    return np.array(holding)


def normal_values(stream_key, extent, scale, reach, shards=(), kind=jnp.bfloat16):
    factor_of = block_scale(stream_key, extent, shards, -0.22, 0.18) if shards else 1.0
    result = jax.random.normal(stream_key, extent, jnp.float32) * scale * factor_of
    return jnp.minimum(jnp.maximum(result, -reach), reach).astype(kind)


def setup_inputs(seed: int = 0) -> dict:
    splits = jax.random.split(jax.random.key(seed), 12)
    control = normal_values(splits[0], (LEV, NLAT, NLON), 1.0, 6.0, ((1, 8), (2, 32)), jnp.float32)
    spread = jnp.clip(jnp.exp(math.log(3.0) - 2.3025851 * jax.random.uniform(splits[1], (LEV, NLAT, NLON), jnp.float32) ** block_scale(splits[1], (LEV, NLAT, NLON), ((1, 8), (2, 32)), -0.2, 0.2)), 0.3, 3.0)
    vert_root = draw_vert_root(jax.random.fold_in(splits[11], 71), 0)
    wind_lon = jnp.clip(jax.random.uniform(splits[3], (LEV, NLAT, NLON), jnp.float32, -0.45, 0.45) * block_scale(splits[3], (LEV, NLAT, NLON), ((0, 32), (1, 8)), -0.4, 0.0), -0.45, 0.45)
    wind_lat = jnp.clip(jax.random.uniform(splits[4], (LEV, NLAT, NLON), jnp.float32, -0.45, 0.45) * block_scale(splits[4], (LEV, NLAT, NLON), ((0, 32), (1, 8)), -0.4, 0.0), -0.45, 0.45)
    obs_dest_keys = jax.random.split(jax.random.fold_in(splits[5], 1), NOBS // NOBS_DEV)
    obs_dest_turns = jax.random.permutation(jax.random.fold_in(splits[5], 3), NOBS // NOBS_DEV)
    obs_dest = jax.vmap(lambda own, number: assign_block(jax.random.fold_in(splits[5], 2), own, number, NOBS_DEV, N_HORIZ, 1, CAP, 2))(obs_dest_keys, obs_dest_turns).reshape((NOBS, 1))
    obs_cells = place_ends(jax.random.randint(splits[6], (4, NOBS), 0, LEV // N_HORIZ * CLAT * NLON), jax.random.fold_in(splits[6], 1), 0, (LEV // N_HORIZ * CLAT * NLON) - 1).astype(jnp.int32)
    obs_time = place_ends(jax.random.randint(splits[7], (NOBS,), 0, NT + 1), jax.random.fold_in(splits[7], 1), 0, NT).astype(jnp.int32)
    obs_value = normal_values(splits[8], (NOBS,), 1.0, 6.0, ((0, 256),), jnp.float32)
    obs_weight = jnp.clip(1.0 * jax.random.uniform(splits[9], (4, NOBS), jnp.float32) ** block_scale(splits[9], (4, NOBS), ((1, 256),), -0.2, 0.2), 0.0, 1.0)
    obs_rinv = jnp.clip(jnp.exp(math.log(3.0) - 2.3025851 * jax.random.uniform(splits[10], (NOBS,), jnp.float32) ** block_scale(splits[10], (NOBS,), ((0, 256),), -0.2, 0.2)), 0.3, 3.0)
    return dict(control=control, spread=spread, vert_root=vert_root, wind_lon=wind_lon, wind_lat=wind_lat, obs_dest=obs_dest, obs_cells=obs_cells, obs_time=obs_time, obs_value=obs_value, obs_weight=obs_weight, obs_rinv=obs_rinv)


def advance(current, west_cells, east_cells, south_rows, north_rows, wind_u, wind_v):
    up_lon = jnp.maximum(wind_u, 0.0)
    down_lon = jnp.minimum(wind_u, 0.0)
    up_lat = jnp.maximum(wind_v, 0.0)
    down_lat = jnp.minimum(wind_v, 0.0)
    return (current - up_lon * (current - west_cells) - down_lon * (east_cells - current)
            - up_lat * (current - south_rows) - down_lat * (north_rows - current))


def forward_step(current, wind_u, wind_v):
    padded = jnp.pad(current, ((0, 0), (1, 1), (0, 0)))
    return advance(current, jnp.roll(current, 1, axis=2), jnp.roll(current, -1, axis=2),
                   padded[:, :-2], padded[:, 2:], wind_u, wind_v)


def adjoint_terms(adjoint_now, wind_u, wind_v):
    up_lon = jnp.maximum(wind_u, 0.0)
    down_lon = jnp.minimum(wind_u, 0.0)
    up_lat = jnp.maximum(wind_v, 0.0)
    down_lat = jnp.minimum(wind_v, 0.0)
    base = (1.0 - up_lon + down_lon - up_lat + down_lat) * adjoint_now
    base = base + jnp.roll(up_lon * adjoint_now, -1, axis=2) - jnp.roll(down_lon * adjoint_now, 1, axis=2)
    return base, up_lat * adjoint_now, down_lat * adjoint_now


def adjoint_step(adjoint_now, wind_u, wind_v):
    base, plus_flux, minus_flux = adjoint_terms(adjoint_now, wind_u, wind_v)
    plus_pad = jnp.pad(plus_flux, ((0, 0), (1, 1), (0, 0)))
    minus_pad = jnp.pad(minus_flux, ((0, 0), (1, 1), (0, 0)))
    return base + plus_pad[:, 2:] - minus_pad[:, :-2]


def reference(control, spread, vert_root, wind_lon, wind_lat, obs_dest, obs_cells, obs_time, obs_value, obs_weight, obs_rinv):
    levels_all, lat_all, lon_all = control.shape
    increment = spread * jnp.dot(vert_root, control.reshape(levels_all, -1), precision=lax.Precision.HIGHEST,
                                 preferred_element_type=jnp.float32).reshape(control.shape)
    states = [increment]
    current = increment
    for tick_index in range(NT):
        current = forward_step(current, wind_lon, wind_lat)
        states.append(current)
    block_size = levels_all * lat_all * lon_all
    states_flat = jnp.stack(states).reshape(-1)
    level_local = LEV // N_HORIZ
    row_ids = jnp.arange(obs_value.shape[0], dtype=jnp.int32)
    band_ids = row_ids // (NOBS_DEV * N_HORIZ)
    group_ids = obs_dest[:, 0]
    level_ids = group_ids[None, :] * level_local + obs_cells // (CLAT * NLON)
    lat_ids = band_ids[None, :] * CLAT + (obs_cells // NLON) % CLAT
    lon_ids = obs_cells % NLON
    global_ids = (level_ids * lat_all + lat_ids) * lon_all + lon_ids
    where_ids = (obs_time[None, :] * block_size + global_ids).astype(jnp.int32)
    picked = states_flat[where_ids]
    hx = jnp.sum(obs_weight * picked, axis=0)
    departure = obs_rinv * (hx - obs_value)
    forcing = jnp.zeros(((NT + 1) * block_size,), jnp.float32).at[where_ids].add(obs_weight * departure[None, :])
    forcing = forcing.reshape(NT + 1, levels_all, lat_all, lon_all)
    adjoint_now = forcing[NT]
    for tick_index in range(NT - 1, -1, -1):
        adjoint_now = adjoint_step(adjoint_now, wind_lon, wind_lat) + forcing[tick_index]
    weighted = (spread * adjoint_now).reshape(levels_all, -1)
    gradient = control + jnp.dot(vert_root.T, weighted, precision=lax.Precision.HIGHEST,
                                 preferred_element_type=jnp.float32).reshape(control.shape)
    return gradient, departure
```

```python
import jax
import jax.numpy as jnp
from jax import lax
from jax.experimental import pallas as pl
from jax.experimental.pallas import tpu as pltpu
from jax.sharding import PartitionSpec as P

NT = 4
CAP = 64
GROUPS = 32
BANDS = 8
LEVELS = 4
TILES = 32
ROWS = TILES * 8
ACCS = 8
MESH = pl.DeviceIdType.MESH
F32 = jnp.float32
I32 = jnp.int32
BF16 = jnp.bfloat16


def in_vmem():
    return pl.BlockSpec(memory_space=pltpu.VMEM)


def in_hbm():
    return pl.BlockSpec(memory_space=pltpu.HBM)


def fetches(sources, targets, sems):
    return [
        pltpu.make_async_copy(source, target, sems.at[index])
        for index, (source, target) in enumerate(zip(sources, targets))
    ]


def split_three(x):
    high = x.astype(BF16)
    rest = x - high.astype(F32)
    middle = rest.astype(BF16)
    low = (rest - middle.astype(F32)).astype(BF16)
    return high, middle, low


def greet(band, group):
    barrier = pltpu.get_barrier_semaphore()

    def peer(step, carry):
        other = lax.rem(group + step, GROUPS)
        pl.semaphore_signal(barrier, inc=1, device_id=(band, other), device_id_type=MESH)
        return carry

    lax.fori_loop(1, GROUPS, peer, 0)

    @pl.when(band > 0)
    def _():
        pl.semaphore_signal(barrier, inc=1, device_id=(band - 1, group), device_id_type=MESH)

    @pl.when(band < BANDS - 1)
    def _():
        pl.semaphore_signal(barrier, inc=1, device_id=(band + 1, group), device_id_type=MESH)


def meet(band):
    sides = (band > 0).astype(I32) + (band < BANDS - 1).astype(I32)
    pl.semaphore_wait(pltpu.get_barrier_semaphore(), GROUPS - 1 + sides)


def to_south(edge, landing, send_sem, recv_sem, index, band, group):
    return pltpu.make_async_remote_copy(
        src_ref=edge.at[index],
        dst_ref=landing.at[index],
        send_sem=send_sem.at[index],
        recv_sem=recv_sem.at[index],
        device_id=(jnp.maximum(band - 1, 0), group),
        device_id_type=MESH,
    )


def to_north(edge, landing, send_sem, recv_sem, index, band, group):
    return pltpu.make_async_remote_copy(
        src_ref=edge.at[index],
        dst_ref=landing.at[index],
        send_sem=send_sem.at[index],
        recv_sem=recv_sem.at[index],
        device_id=(jnp.minimum(band + 1, BANDS - 1), group),
        device_id_type=MESH,
    )


class Rims:
    def __init__(self, band, group, refs):
        self.band, self.group = band, group
        (
            self.edge_south,
            self.edge_north,
            self.halo_south,
            self.halo_north,
            self.send_south,
            self.send_north,
            self.recv_south,
            self.recv_north,
        ) = refs

    @staticmethod
    def scratch():
        steps = NT * LEVELS
        edges = pltpu.VMEM((steps + LEVELS, TILES, 128), F32)
        halos = pltpu.VMEM((steps, TILES, 128), F32)
        sems = pltpu.SemaphoreType.DMA((steps,))
        return [edges] * 2 + [halos] * 2 + [sems] * 4

    def clear(self):
        @pl.when(self.band == 0)
        def _():
            self.halo_south[...] = jnp.zeros_like(self.halo_south)

        @pl.when(self.band == BANDS - 1)
        def _():
            self.halo_north[...] = jnp.zeros_like(self.halo_north)

    def south(self, index):
        return to_south(
            self.edge_south, self.halo_north, self.send_south, self.recv_north,
            index, self.band, self.group,
        )

    def north(self, index):
        return to_north(
            self.edge_north, self.halo_south, self.send_north, self.recv_south,
            index, self.band, self.group,
        )

    def start(self, index):
        @pl.when(self.band > 0)
        def _():
            self.south(index).start()

        @pl.when(self.band < BANDS - 1)
        def _():
            self.north(index).start()

    def wait(self, index):
        @pl.when(self.band > 0)
        def _():
            self.north(index).wait_recv()

        @pl.when(self.band < BANDS - 1)
        def _():
            self.south(index).wait_recv()

    def drain(self):
        def one(index, carry):
            @pl.when(self.band > 0)
            def _():
                self.south(index).wait_send()

            @pl.when(self.band < BANDS - 1)
            def _():
                self.north(index).wait_send()

            return carry

        lax.fori_loop(0, NT * LEVELS, one, 0)


def for_peers(group, act):
    def one(step, carry):
        act(lax.rem(group + step, GROUPS))
        return carry

    lax.fori_loop(1, GROUPS, one, 0)


def forward_kernel(
    control_in, spread_in, vert_root_in, wind_lon_in, wind_lat_in, dest_in,
    cells_in, time_in, value_in, weight_in, rinv_in,
    states, received, rows, slots, wind_lon, wind_lat, dest,
    control, spread, vert_root, cells, time, value, weight, rinv, load_sems,
    increment, payload, field_send, field_recv, obs_send, obs_recv, *rim_refs,
):
    band, group = lax.axis_index("obs"), lax.axis_index("horiz")
    rims = Rims(band, group, rim_refs)
    loads = fetches(
        (
            control_in, vert_root_in, spread_in, dest_in, cells_in, time_in, value_in,
            weight_in, rinv_in, wind_lon_in, wind_lat_in,
        ),
        (
            control, vert_root, spread, dest, cells, time, value, weight, rinv,
            wind_lon, wind_lat,
        ),
        load_sems,
    )
    for load in loads:
        load.start()
    greet(band, group)
    rims.clear()
    for load in loads[:3]:
        load.wait()
    root = vert_root[...]
    for lat in range(8):
        column = control[:, lat, :]
        mixed = jnp.dot(
            root, column, precision=lax.Precision.HIGHEST, preferred_element_type=F32
        )
        increment[:, lat, :] = spread[:, lat, :] * mixed
    meet(band)

    def field_copy(target, source):
        return pltpu.make_async_remote_copy(
            src_ref=increment.at[pl.ds(LEVELS * target, LEVELS)],
            dst_ref=states.at[pl.ds(0, LEVELS), source],
            send_sem=field_send.at[target],
            recv_sem=field_recv.at[source],
            device_id=(band, target),
            device_id_type=MESH,
        )

    def obs_copy(target, source):
        return pltpu.make_async_remote_copy(
            src_ref=payload.at[target],
            dst_ref=received.at[source],
            send_sem=obs_send.at[target],
            recv_sem=obs_recv.at[source],
            device_id=(band, target),
            device_id_type=MESH,
        )

    for_peers(group, lambda peer: field_copy(peer, group).start())
    for level in range(LEVELS):
        states[level, group] = increment[LEVELS * group + level]

    for load in loads[3:]:
        load.wait()
    owner = dest[...]
    hit = lax.broadcasted_iota(I32, (GROUPS, 1024), 0) == owner
    hit_f = jnp.where(hit, 1.0, 0.0)
    hit_b = hit_f.astype(BF16)
    earlier = (
        lax.broadcasted_iota(I32, (128, 128), 0) < lax.broadcasted_iota(I32, (128, 128), 1)
    )
    earlier = jnp.where(earlier, 1.0, 0.0).astype(BF16)
    carried = jnp.zeros((GROUPS, 1), F32)
    for chunk in range(8):
        at = slice(chunk * 128, chunk * 128 + 128)
        before = jnp.dot(hit_b[:, at], earlier, preferred_element_type=F32) + carried
        slots[:, at] = jnp.sum(hit_f[:, at] * before, axis=0, keepdims=True).astype(I32)
        carried = carried + jnp.sum(hit_f[:, at], axis=1, keepdims=True)
    place = lax.broadcasted_iota(I32, (128, 1024), 0)
    slot_hit = (place & (CAP - 1)) == slots[...]
    first_half = place < CAP
    first_slot = jnp.logical_and(slot_hit, first_half)
    second_slot = jnp.logical_and(slot_hit, jnp.logical_not(first_half))
    fields = []
    for k in range(4):
        cell = cells[k : k + 1, :]
        row = (
            (time[...] * LEVELS + (cell >> 15)) * ROWS
            + ((cell & 4095) >> 7) * 8
            + ((cell >> 12) & 7)
        )
        fields.append(((row * 128 + (cell & 127)).astype(F32), weight[k : k + 1, :]))
    fields.append((value[...], rinv[...]))
    payload[...] = jnp.zeros_like(payload)
    for index, (first, second) in enumerate(fields):
        total = None
        for one, two in zip(split_three(first), split_three(second)):
            chosen = jnp.where(
                first_slot, one.astype(F32), jnp.where(second_slot, two.astype(F32), 0.0)
            ).astype(BF16)
            term = lax.dot_general(
                hit_b, chosen, (((1,), (1,)), ((), ())), preferred_element_type=F32
            )
            total = term if total is None else total + term
        payload[:, index, :] = total
    for_peers(group, lambda peer: obs_copy(peer, group).start())
    received[group] = payload[group]

    for_peers(group, lambda peer: field_copy(group, peer).wait_recv())
    for level in range(LEVELS):
        for tile in range(TILES):
            cell = states[level, tile]
            rims.edge_south[level, tile : tile + 1, :] = cell[0:1, :]
            rims.edge_north[level, tile : tile + 1, :] = cell[7:8, :]
        rims.start(level)

    lane = lax.broadcasted_iota(I32, (8, 128), 1)
    lat = lax.broadcasted_iota(I32, (8, 128), 0)

    def advance(index, carry):
        level = lax.rem(index, LEVELS)
        rims.wait(index)

        def tile_of(tile):
            now = states[index, tile % TILES]
            return now, pltpu.roll(now, 1, 1), pltpu.roll(now, 127, 1)

        before, here = tile_of(TILES - 1), tile_of(0)
        for tile in range(TILES):
            after = tile_of(tile + 1)
            now = here[0]
            west = jnp.where(lane == 0, before[1], here[1])
            east = jnp.where(lane == 127, after[2], here[2])
            south = jnp.where(
                lat == 0, rims.halo_south[index, tile : tile + 1, :], pltpu.roll(now, 1, 0)
            )
            north = jnp.where(
                lat == 7, rims.halo_north[index, tile : tile + 1, :], pltpu.roll(now, 7, 0)
            )
            at = slice(tile * 128, tile * 128 + 128)
            lon, lati = wind_lon[level, :, at], wind_lat[level, :, at]
            new = (
                now
                - jnp.maximum(lon, 0.0) * (now - west)
                - jnp.minimum(lon, 0.0) * (east - now)
                - jnp.maximum(lati, 0.0) * (now - south)
                - jnp.minimum(lati, 0.0) * (north - now)
            )
            states[index + LEVELS, tile] = new

            rims.edge_south[index + LEVELS, tile : tile + 1, :] = new[0:1, :]
            rims.edge_north[index + LEVELS, tile : tile + 1, :] = new[7:8, :]
            before, here = here, after

        @pl.when(index < (NT - 1) * LEVELS)
        def _():
            rims.start(index + LEVELS)

        return carry

    lax.fori_loop(0, NT * LEVELS, advance, 0)

    for_peers(group, lambda peer: obs_copy(group, peer).wait_recv())
    for sender in range(GROUPS):
        rows[sender * 8 : sender * 8 + 8, :] = received[sender].astype(I32) >> 7
    for_peers(group, lambda peer: field_copy(peer, group).wait_send())
    for_peers(group, lambda peer: obs_copy(peer, group).wait_send())
    rims.drain()


def obs_kernel(rows, received, states, forcing, departure, picked, placed, *sums):
    for one in sums:
        one[...] = jnp.zeros_like(one)
    lane = lax.broadcasted_iota(I32, (CAP, 128), 1)
    place = lax.broadcasted_iota(I32, (CAP, 128), 0)

    def block(sender, carry):
        flipped = received[sender].T
        for k in range(4):
            for s in range(CAP):
                row = rows[sender * 8 + k, s]
                picked[k * CAP + s : k * CAP + s + 1, :] = states[pl.ds(row, 1), :]
        hits, total = [], None
        for k in range(4):
            where = flipped[0:CAP, k : k + 1].astype(I32) & 127
            hits.append(jnp.where(lane == where, flipped[CAP:, k : k + 1], 0.0))
            term = hits[k] * picked[k * CAP : k * CAP + CAP, :]
            total = term if total is None else total + term
        hx = jnp.sum(total, axis=1, keepdims=True)
        weighted = flipped[CAP:, 4:5] * (hx - flipped[0:CAP, 4:5])
        for k in range(4):
            placed[k * CAP : k * CAP + CAP, :] = hits[k] * weighted
        departure[sender] = jnp.sum(
            jnp.where(lane == place, weighted, 0.0), axis=0, keepdims=True
        )
        for s in range(CAP):
            for k in range(4):
                one = sums[(s * 4 + k) % ACCS]
                row = rows[sender * 8 + k, s]
                one[pl.ds(row, 1), :] += placed[k * CAP + s : k * CAP + s + 1, :]
        return carry

    lax.fori_loop(0, GROUPS, block, 0)

    def add(index, carry):
        at = pl.ds(pl.multiple_of(index * 64, 64), 64)
        total = sums[0][at, :]
        for one in sums[1:]:
            total = total + one[at, :]
        forcing[at, :] = total
        return carry

    lax.fori_loop(0, (NT + 1) * LEVELS * ROWS // 64, add, 0)


def adjoint_kernel(
    control_in, spread_in, vert_root_in, wind_lon, wind_lat, forcing, owner_dep, dest, slots,
    gradient, departure,
    control, spread, vert_root, load_sems,
    adjoint, column, returned, field_send, field_recv, dep_send, dep_recv, *rim_refs,
):
    band, group = lax.axis_index("obs"), lax.axis_index("horiz")
    rims = Rims(band, group, rim_refs)
    loads = fetches(
        (control_in, spread_in, vert_root_in), (control, spread, vert_root), load_sems
    )
    for load in loads:
        load.start()
    greet(band, group)
    rims.clear()
    for level in range(LEVELS):
        for tile in range(TILES):
            at = slice(tile * 128, tile * 128 + 128)
            now = forcing[NT * LEVELS + level, tile]
            lati = wind_lat[level, :, at]
            adjoint[level, tile] = now
            rims.edge_south[level, tile : tile + 1, :] = (jnp.maximum(lati, 0.0) * now)[0:1, :]
            rims.edge_north[level, tile : tile + 1, :] = (jnp.minimum(lati, 0.0) * now)[7:8, :]
    meet(band)
    for level in range(LEVELS):
        rims.start(level)

    def dep_copy(target, source):
        return pltpu.make_async_remote_copy(
            src_ref=owner_dep.at[target],
            dst_ref=returned.at[source],
            send_sem=dep_send.at[target],
            recv_sem=dep_recv.at[source],
            device_id=(band, target),
            device_id_type=MESH,
        )

    def field_copy(target, source):
        return pltpu.make_async_remote_copy(
            src_ref=adjoint.at[pl.ds(NT * LEVELS, LEVELS), target],
            dst_ref=column.at[pl.ds(LEVELS * source, LEVELS)],
            send_sem=field_send.at[target],
            recv_sem=field_recv.at[source],
            device_id=(band, target),
            device_id_type=MESH,
        )

    for_peers(group, lambda peer: dep_copy(peer, group).start())
    returned[group] = owner_dep[group]

    lane = lax.broadcasted_iota(I32, (8, 128), 1)
    lat = lax.broadcasted_iota(I32, (8, 128), 0)

    def retreat(index, carry):
        level = lax.rem(index, LEVELS)
        step = lax.div(index, LEVELS)
        rims.wait(index)

        def tile_of(tile):
            tile = tile % TILES
            at = slice(tile * 128, tile * 128 + 128)
            now = adjoint[index, tile]
            lon = wind_lon[level, :, at]
            up, down = jnp.maximum(lon, 0.0), jnp.minimum(lon, 0.0)
            return (
                now,
                1.0 - up + down,
                pltpu.roll(up * now, 127, 1),
                pltpu.roll(down * now, 1, 1),
            )

        before, here = tile_of(TILES - 1), tile_of(0)
        for tile in range(TILES):
            after = tile_of(tile + 1)
            at = slice(tile * 128, tile * 128 + 128)
            now = here[0]
            lati = wind_lat[level, :, at]
            up, down = jnp.maximum(lati, 0.0), jnp.minimum(lati, 0.0)
            from_east = jnp.where(lane == 127, after[2], here[2])
            from_west = jnp.where(lane == 0, before[3], here[3])
            from_north = jnp.where(
                lat == 7, rims.halo_north[index, tile : tile + 1, :], pltpu.roll(up * now, 7, 0)
            )
            from_south = jnp.where(
                lat == 0, rims.halo_south[index, tile : tile + 1, :], pltpu.roll(down * now, 1, 0)
            )
            new = (
                (here[1] - up + down) * now
                + from_east
                - from_west
                + from_north
                - from_south
                + forcing[(NT - 1 - step) * LEVELS + level, tile]
            )
            adjoint[index + LEVELS, tile] = new

            rims.edge_south[index + LEVELS, tile : tile + 1, :] = (up * new)[0:1, :]
            rims.edge_north[index + LEVELS, tile : tile + 1, :] = (down * new)[7:8, :]
            before, here = here, after

        @pl.when(index < (NT - 1) * LEVELS)
        def _():
            rims.start(index + LEVELS)

        return carry

    lax.fori_loop(0, NT * LEVELS, retreat, 0)

    for_peers(group, lambda peer: field_copy(peer, group).start())
    for level in range(LEVELS):
        column[LEVELS * group + level] = adjoint[NT * LEVELS + level, group]

    for_peers(group, lambda peer: dep_copy(group, peer).wait_recv())
    hit = lax.broadcasted_iota(I32, (GROUPS, 1024), 0) == dest[...]
    hit = jnp.where(hit, 1.0, 0.0).astype(BF16)
    spread_out = None
    for part in split_three(returned[:, 0, :]):
        term = lax.dot_general(
            part, hit, (((0,), (0,)), ((), ())), preferred_element_type=F32
        )
        spread_out = term if spread_out is None else spread_out + term
    place = lax.broadcasted_iota(I32, (128, 1024), 0)
    departure[...] = jnp.sum(
        jnp.where(place == slots[...], spread_out, 0.0), axis=0, keepdims=True
    )

    for load in loads:
        load.wait()
    root = vert_root[...].T
    for_peers(group, lambda peer: field_copy(group, peer).wait_recv())
    for lat_row in range(8):
        weighted = spread[:, lat_row, :] * column[:, lat_row, :]
        mixed = jnp.dot(
            root, weighted, precision=lax.Precision.HIGHEST, preferred_element_type=F32
        )
        gradient[:, lat_row, :] = control[:, lat_row, :] + mixed
    for_peers(group, lambda peer: field_copy(peer, group).wait_send())
    for_peers(group, lambda peer: dep_copy(peer, group).wait_send())
    rims.drain()


def per_device(
    control, spread, vert_root, wind_lon, wind_lat,
    obs_dest, obs_cells, obs_time, obs_value, obs_weight, obs_rinv,
):
    count = obs_time.shape[0]
    dest = obs_dest.reshape(1, count)
    fields = (NT + 1) * LEVELS
    wide, long = control.shape, (LEVELS, 8, TILES * 128)
    states, received, rows, slots, lon, lat, owner = pl.pallas_call(
        forward_kernel,
        out_shape=(
            jax.ShapeDtypeStruct((fields, TILES, 8, 128), F32),
            jax.ShapeDtypeStruct((GROUPS, 8, 128), F32),
            jax.ShapeDtypeStruct((GROUPS * 8, 128), I32),
            jax.ShapeDtypeStruct((1, count), I32),
            jax.ShapeDtypeStruct(long, F32),
            jax.ShapeDtypeStruct(long, F32),
            jax.ShapeDtypeStruct((1, count), I32),
        ),
        in_specs=[in_hbm()] * 11,
        out_specs=(in_vmem(),) * 7,
        scratch_shapes=[
            pltpu.VMEM(wide, F32),
            pltpu.VMEM(wide, F32),
            pltpu.VMEM((128, 128), F32),
            pltpu.VMEM((4, count), I32),
            pltpu.VMEM((1, count), I32),
            pltpu.VMEM((1, count), F32),
            pltpu.VMEM((4, count), F32),
            pltpu.VMEM((1, count), F32),
            pltpu.SemaphoreType.DMA((11,)),
            pltpu.VMEM(wide, F32),
            pltpu.VMEM((GROUPS, 8, 128), F32),
        ]
        + [pltpu.SemaphoreType.DMA((GROUPS,))] * 4
        + Rims.scratch(),
        compiler_params=pltpu.CompilerParams(
            collective_id=0, has_side_effects=True, vmem_limit_bytes=48 << 20
        ),
        name="forward",
    )(
        control, spread, vert_root, wind_lon, wind_lat, dest, obs_cells,
        obs_time.reshape(1, count), obs_value.reshape(1, count), obs_weight,
        obs_rinv.reshape(1, count),
    )
    forcing, owner_dep = pl.pallas_call(
        obs_kernel,
        out_shape=(
            jax.ShapeDtypeStruct((fields * ROWS, 128), F32),
            jax.ShapeDtypeStruct((GROUPS, 1, 128), F32),
        ),
        in_specs=[pl.BlockSpec(memory_space=pltpu.SMEM), in_vmem(), in_vmem()],
        out_specs=(in_vmem(),) * 2,
        scratch_shapes=[pltpu.VMEM((4 * CAP, 128), F32)] * 2
        + [pltpu.VMEM((fields * ROWS, 128), F32)] * ACCS,
        compiler_params=pltpu.CompilerParams(vmem_limit_bytes=48 << 20),
        name="observe",
    )(rows, received, states.reshape(fields * ROWS, 128))
    gradient, departure = pl.pallas_call(
        adjoint_kernel,
        out_shape=(
            jax.ShapeDtypeStruct(control.shape, F32),
            jax.ShapeDtypeStruct((1, count), F32),
        ),
        in_specs=[in_hbm()] * 3 + [in_vmem()] * 6,
        out_specs=(in_vmem(),) * 2,
        scratch_shapes=[
            pltpu.VMEM(wide, F32),
            pltpu.VMEM(wide, F32),
            pltpu.VMEM((128, 128), F32),
            pltpu.SemaphoreType.DMA((3,)),
            pltpu.VMEM((fields, TILES, 8, 128), F32),
            pltpu.VMEM((128, 8, 128), F32),
            pltpu.VMEM((GROUPS, 1, 128), F32),
        ]
        + [pltpu.SemaphoreType.DMA((GROUPS,))] * 4
        + Rims.scratch(),
        compiler_params=pltpu.CompilerParams(
            collective_id=1, has_side_effects=True, vmem_limit_bytes=48 << 20
        ),
        name="retreat",
    )(
        control, spread, vert_root, lon, lat,
        forcing.reshape(fields, TILES, 8, 128), owner_dep, owner, slots,
    )
    return gradient, departure.reshape(count)


def solution(mesh):
    in_specs = (
        P(None, "obs", "horiz"),
        P(None, "obs", "horiz"),
        P(),
        P("horiz", "obs", None),
        P("horiz", "obs", None),
        P(("obs", "horiz"), None),
        P(None, ("obs", "horiz")),
        P(("obs", "horiz")),
        P(("obs", "horiz")),
        P(None, ("obs", "horiz")),
        P(("obs", "horiz")),
    )
    out_specs = (P(None, "obs", "horiz"), P(("obs", "horiz")))
    return jax.shard_map(
        per_device, mesh=mesh, in_specs=in_specs, out_specs=out_specs, check_vma=False
    )
```

```python
import jax
import jax.numpy as jnp
from jax import lax
from jax.experimental import pallas as pl
from jax.experimental.pallas import tpu as pltpu
from jax.sharding import PartitionSpec as P

NT = 4
CAP = 64
GROUPS = 32
BANDS = 8
LEVELS = 4
TILES = 32
ROWS = TILES * 8
ACCS = 8
MESH = pl.DeviceIdType.MESH
F32 = jnp.float32
I32 = jnp.int32
BF16 = jnp.bfloat16


def in_vmem():
    return pl.BlockSpec(memory_space=pltpu.VMEM)


def in_hbm():
    return pl.BlockSpec(memory_space=pltpu.HBM)


def stay(x):
    return pltpu.with_memory_space_constraint(x, pltpu.HBM)


def fetches(sources, targets, sems):
    return [
        pltpu.make_async_copy(source, target, sems.at[index])
        for index, (source, target) in enumerate(zip(sources, targets))
    ]


def split_three(x):
    high = x.astype(BF16)
    rest = x - high.astype(F32)
    middle = rest.astype(BF16)
    low = (rest - middle.astype(F32)).astype(BF16)
    return high, middle, low


def greet(band, group):
    barrier = pltpu.get_barrier_semaphore()

    def peer(step, carry):
        other = lax.rem(group + step, GROUPS)
        pl.semaphore_signal(barrier, inc=1, device_id=(band, other), device_id_type=MESH)
        return carry

    lax.fori_loop(1, GROUPS, peer, 0)

    @pl.when(band > 0)
    def _():
        pl.semaphore_signal(barrier, inc=1, device_id=(band - 1, group), device_id_type=MESH)

    @pl.when(band < BANDS - 1)
    def _():
        pl.semaphore_signal(barrier, inc=1, device_id=(band + 1, group), device_id_type=MESH)


def meet(band):
    sides = (band > 0).astype(I32) + (band < BANDS - 1).astype(I32)
    pl.semaphore_wait(pltpu.get_barrier_semaphore(), GROUPS - 1 + sides)


def to_south(edge, landing, send_sem, recv_sem, index, band, group):
    return pltpu.make_async_remote_copy(
        src_ref=edge.at[index],
        dst_ref=landing.at[index],
        send_sem=send_sem.at[index],
        recv_sem=recv_sem.at[index],
        device_id=(jnp.maximum(band - 1, 0), group),
        device_id_type=MESH,
    )


def to_north(edge, landing, send_sem, recv_sem, index, band, group):
    return pltpu.make_async_remote_copy(
        src_ref=edge.at[index],
        dst_ref=landing.at[index],
        send_sem=send_sem.at[index],
        recv_sem=recv_sem.at[index],
        device_id=(jnp.minimum(band + 1, BANDS - 1), group),
        device_id_type=MESH,
    )


class Rims:
    def __init__(self, band, group, refs):
        self.band, self.group = band, group
        (
            self.edge_south,
            self.edge_north,
            self.halo_south,
            self.halo_north,
            self.send_south,
            self.send_north,
            self.recv_south,
            self.recv_north,
        ) = refs

    @staticmethod
    def scratch():
        steps = NT * LEVELS
        edges = pltpu.VMEM((steps + LEVELS, TILES, 128), F32)
        halos = pltpu.VMEM((steps, TILES, 128), F32)
        sems = pltpu.SemaphoreType.DMA((steps,))
        return [edges] * 2 + [halos] * 2 + [sems] * 4

    def clear(self):
        @pl.when(self.band == 0)
        def _():
            self.halo_south[...] = jnp.zeros_like(self.halo_south)

        @pl.when(self.band == BANDS - 1)
        def _():
            self.halo_north[...] = jnp.zeros_like(self.halo_north)

    def south(self, index):
        return to_south(
            self.edge_south, self.halo_north, self.send_south, self.recv_north,
            index, self.band, self.group,
        )

    def north(self, index):
        return to_north(
            self.edge_north, self.halo_south, self.send_north, self.recv_south,
            index, self.band, self.group,
        )

    def start(self, index):
        @pl.when(self.band > 0)
        def _():
            self.south(index).start()

        @pl.when(self.band < BANDS - 1)
        def _():
            self.north(index).start()

    def wait(self, index):
        @pl.when(self.band > 0)
        def _():
            self.north(index).wait_recv()

        @pl.when(self.band < BANDS - 1)
        def _():
            self.south(index).wait_recv()

    def drain(self):
        def one(index, carry):
            @pl.when(self.band > 0)
            def _():
                self.south(index).wait_send()

            @pl.when(self.band < BANDS - 1)
            def _():
                self.north(index).wait_send()

            return carry

        lax.fori_loop(0, NT * LEVELS, one, 0)


def for_peers(group, act):
    def one(step, carry):
        act(lax.rem(group + step, GROUPS))
        return carry

    lax.fori_loop(1, GROUPS, one, 0)


def forward_kernel(
    control_in, spread_in, vert_root_in, wind_lon_in, wind_lat_in, dest_in,
    cells_in, time_in, value_in, weight_in, rinv_in,
    states, received, rows, slots, wind_lon, wind_lat, dest,
    control, spread, vert_root, cells, time, value, weight, rinv, load_sems,
    increment, payload, field_send, field_recv, obs_send, obs_recv, *rim_refs,
):
    band, group = lax.axis_index("obs"), lax.axis_index("horiz")
    rims = Rims(band, group, rim_refs)
    loads = fetches(
        (
            control_in, vert_root_in, spread_in, dest_in, cells_in, time_in, value_in,
            weight_in, rinv_in, wind_lon_in, wind_lat_in,
        ),
        (
            control, vert_root, spread, dest, cells, time, value, weight, rinv,
            wind_lon, wind_lat,
        ),
        load_sems,
    )
    for load in loads:
        load.start()
    greet(band, group)
    rims.clear()
    for load in loads[:3]:
        load.wait()
    root = vert_root[...]
    for lat in range(8):
        column = control[:, lat, :]
        mixed = jnp.dot(
            root, column, precision=lax.Precision.HIGHEST, preferred_element_type=F32
        )
        increment[:, lat, :] = spread[:, lat, :] * mixed
    meet(band)

    def field_copy(target, source):
        return pltpu.make_async_remote_copy(
            src_ref=increment.at[pl.ds(LEVELS * target, LEVELS)],
            dst_ref=states.at[pl.ds(0, LEVELS), source],
            send_sem=field_send.at[target],
            recv_sem=field_recv.at[source],
            device_id=(band, target),
            device_id_type=MESH,
        )

    def obs_copy(target, source):
        return pltpu.make_async_remote_copy(
            src_ref=payload.at[target],
            dst_ref=received.at[source],
            send_sem=obs_send.at[target],
            recv_sem=obs_recv.at[source],
            device_id=(band, target),
            device_id_type=MESH,
        )

    for_peers(group, lambda peer: field_copy(peer, group).start())
    for level in range(LEVELS):
        states[level, group] = increment[LEVELS * group + level]

    for load in loads[3:]:
        load.wait()
    owner = dest[...]
    hit = lax.broadcasted_iota(I32, (GROUPS, 1024), 0) == owner
    hit_f = jnp.where(hit, 1.0, 0.0)
    hit_b = hit_f.astype(BF16)
    earlier = (
        lax.broadcasted_iota(I32, (128, 128), 0) < lax.broadcasted_iota(I32, (128, 128), 1)
    )
    earlier = jnp.where(earlier, 1.0, 0.0).astype(BF16)
    carried = jnp.zeros((GROUPS, 1), F32)
    for chunk in range(8):
        at = slice(chunk * 128, chunk * 128 + 128)
        before = jnp.dot(hit_b[:, at], earlier, preferred_element_type=F32) + carried
        slots[:, at] = jnp.sum(hit_f[:, at] * before, axis=0, keepdims=True).astype(I32)
        carried = carried + jnp.sum(hit_f[:, at], axis=1, keepdims=True)
    place = lax.broadcasted_iota(I32, (128, 1024), 0)
    slot_hit = (place & (CAP - 1)) == slots[...]
    first_half = place < CAP
    first_slot = jnp.logical_and(slot_hit, first_half)
    second_slot = jnp.logical_and(slot_hit, jnp.logical_not(first_half))
    fields = []
    for k in range(4):
        cell = cells[k : k + 1, :]
        row = (
            (time[...] * LEVELS + (cell >> 15)) * ROWS
            + ((cell & 4095) >> 7) * 8
            + ((cell >> 12) & 7)
        )
        fields.append(((row * 128 + (cell & 127)).astype(F32), weight[k : k + 1, :]))
    fields.append((value[...], rinv[...]))
    payload[...] = jnp.zeros_like(payload)
    for index, (first, second) in enumerate(fields):
        total = None
        for one, two in zip(split_three(first), split_three(second)):
            chosen = jnp.where(
                first_slot, one.astype(F32), jnp.where(second_slot, two.astype(F32), 0.0)
            ).astype(BF16)
            term = lax.dot_general(
                hit_b, chosen, (((1,), (1,)), ((), ())), preferred_element_type=F32
            )
            total = term if total is None else total + term
        payload[:, index, :] = total
    for_peers(group, lambda peer: obs_copy(peer, group).start())
    received[group] = payload[group]

    for_peers(group, lambda peer: field_copy(group, peer).wait_recv())
    for level in range(LEVELS):
        for tile in range(TILES):
            cell = states[level, tile]
            rims.edge_south[level, tile : tile + 1, :] = cell[0:1, :]
            rims.edge_north[level, tile : tile + 1, :] = cell[7:8, :]
        rims.start(level)

    lane = lax.broadcasted_iota(I32, (8, 128), 1)
    lat = lax.broadcasted_iota(I32, (8, 128), 0)

    def advance(index, carry):
        level = lax.rem(index, LEVELS)
        rims.wait(index)

        def tile_of(tile):
            now = states[index, tile % TILES]
            return now, pltpu.roll(now, 1, 1), pltpu.roll(now, 127, 1)

        before, here = tile_of(TILES - 1), tile_of(0)
        for tile in range(TILES):
            after = tile_of(tile + 1)
            now = here[0]
            west = jnp.where(lane == 0, before[1], here[1])
            east = jnp.where(lane == 127, after[2], here[2])
            south = jnp.where(
                lat == 0, rims.halo_south[index, tile : tile + 1, :], pltpu.roll(now, 1, 0)
            )
            north = jnp.where(
                lat == 7, rims.halo_north[index, tile : tile + 1, :], pltpu.roll(now, 7, 0)
            )
            at = slice(tile * 128, tile * 128 + 128)
            lon, lati = wind_lon[level, :, at], wind_lat[level, :, at]
            new = (
                now
                - jnp.maximum(lon, 0.0) * (now - west)
                - jnp.minimum(lon, 0.0) * (east - now)
                - jnp.maximum(lati, 0.0) * (now - south)
                - jnp.minimum(lati, 0.0) * (north - now)
            )
            states[index + LEVELS, tile] = new

            rims.edge_south[index + LEVELS, tile : tile + 1, :] = new[0:1, :]
            rims.edge_north[index + LEVELS, tile : tile + 1, :] = new[7:8, :]
            before, here = here, after

        @pl.when(index < (NT - 1) * LEVELS)
        def _():
            rims.start(index + LEVELS)

        return carry

    lax.fori_loop(0, NT * LEVELS, advance, 0)

    for_peers(group, lambda peer: obs_copy(group, peer).wait_recv())
    for sender in range(GROUPS):
        rows[sender * 8 : sender * 8 + 8, :] = received[sender].astype(I32) >> 7
    for_peers(group, lambda peer: field_copy(peer, group).wait_send())
    for_peers(group, lambda peer: obs_copy(peer, group).wait_send())
    rims.drain()


def obs_kernel(
    rows, received, states, forcing, departure, picked, placed, indices, index_sems, *sums
):
    lane = lax.broadcasted_iota(I32, (CAP, 128), 1)
    place = lax.broadcasted_iota(I32, (CAP, 128), 0)
    size = 4 * CAP

    def fetch(sender, side):
        at = pl.ds(pl.multiple_of(jnp.minimum(sender, GROUPS - 1) * 8, 8), 8)
        return pltpu.make_async_copy(rows.at[at], indices.at[side], index_sems.at[side])

    def gather(k, s, side):
        row = indices[side, k, s]
        picked[k * CAP + s : k * CAP + s + 1, :] = states[pl.ds(row, 1), :]

    def scatter(k, s, side):
        one = sums[(s * 4 + k) % ACCS]
        at = (side % 2) * size + k * CAP + s
        row = indices[side, k, s]
        one[pl.ds(row, 1), :] += placed[at : at + 1, :]

    def weigh(sender, side):
        flipped = received[sender].T
        hits, total = [], None
        for k in range(4):
            where = flipped[0:CAP, k : k + 1].astype(I32) & 127
            hits.append(jnp.where(lane == where, flipped[CAP:, k : k + 1], 0.0))
            term = hits[k] * picked[k * CAP : k * CAP + CAP, :]
            total = term if total is None else total + term
        hx = jnp.sum(total, axis=1, keepdims=True)
        weighted = flipped[CAP:, 4:5] * (hx - flipped[0:CAP, 4:5])
        for k in range(4):
            at = (side % 2) * size + k * CAP
            placed[at : at + CAP, :] = hits[k] * weighted
        departure[sender] = jnp.sum(
            jnp.where(lane == place, weighted, 0.0), axis=0, keepdims=True
        )

    for side in range(4):
        fetch(side, side).start()
    for one in sums:
        one[...] = jnp.zeros_like(one)
    fetch(0, 0).wait()
    for s in range(CAP):
        for k in range(4):
            gather(k, s, 0)
    weigh(0, 0)

    def four(index, carry):
        for side in range(4):
            sender, ahead = 4 * index + side, (side + 1) % 4
            fetch(sender + 1, ahead).wait()
            for s in range(CAP):
                for k in range(4):
                    gather(k, s, ahead)
                    scatter(k, s, side)
            weigh(jnp.minimum(sender + 1, GROUPS - 1), ahead)
            fetch(sender + 4, side).start()
        return carry

    lax.fori_loop(0, GROUPS // 4, four, 0)
    for side in range(1, 4):
        fetch(GROUPS + side, side).wait()

    def add(index, carry):
        at = pl.ds(pl.multiple_of(index * 64, 64), 64)
        total = sums[0][at, :]
        for one in sums[1:]:
            total = total + one[at, :]
        forcing[at, :] = total
        return carry

    lax.fori_loop(0, (NT + 1) * LEVELS * ROWS // 64, add, 0)


def adjoint_kernel(
    control_in, spread_in, vert_root_in, wind_lon, wind_lat, forcing, owner_dep, dest, slots,
    gradient, departure,
    control, spread, vert_root, load_sems,
    adjoint, column, returned, field_send, field_recv, dep_send, dep_recv, *rim_refs,
):
    band, group = lax.axis_index("obs"), lax.axis_index("horiz")
    rims = Rims(band, group, rim_refs)
    loads = fetches(
        (control_in, spread_in, vert_root_in), (control, spread, vert_root), load_sems
    )
    for load in loads:
        load.start()
    greet(band, group)
    rims.clear()
    for level in range(LEVELS):
        for tile in range(TILES):
            at = slice(tile * 128, tile * 128 + 128)
            now = forcing[NT * LEVELS + level, tile]
            lati = wind_lat[level, :, at]
            adjoint[level, tile] = now
            rims.edge_south[level, tile : tile + 1, :] = (jnp.maximum(lati, 0.0) * now)[0:1, :]
            rims.edge_north[level, tile : tile + 1, :] = (jnp.minimum(lati, 0.0) * now)[7:8, :]
    meet(band)
    for level in range(LEVELS):
        rims.start(level)

    def dep_copy(target, source):
        return pltpu.make_async_remote_copy(
            src_ref=owner_dep.at[target],
            dst_ref=returned.at[source],
            send_sem=dep_send.at[target],
            recv_sem=dep_recv.at[source],
            device_id=(band, target),
            device_id_type=MESH,
        )

    def field_copy(target, source):
        return pltpu.make_async_remote_copy(
            src_ref=adjoint.at[pl.ds(NT * LEVELS, LEVELS), target],
            dst_ref=column.at[pl.ds(LEVELS * source, LEVELS)],
            send_sem=field_send.at[target],
            recv_sem=field_recv.at[source],
            device_id=(band, target),
            device_id_type=MESH,
        )

    for_peers(group, lambda peer: dep_copy(peer, group).start())
    returned[group] = owner_dep[group]

    lane = lax.broadcasted_iota(I32, (8, 128), 1)
    lat = lax.broadcasted_iota(I32, (8, 128), 0)

    def retreat(index, carry):
        level = lax.rem(index, LEVELS)
        step = lax.div(index, LEVELS)
        rims.wait(index)

        def tile_of(tile):
            tile = tile % TILES
            at = slice(tile * 128, tile * 128 + 128)
            now = adjoint[index, tile]
            lon = wind_lon[level, :, at]
            up, down = jnp.maximum(lon, 0.0), jnp.minimum(lon, 0.0)
            return (
                now,
                1.0 - up + down,
                pltpu.roll(up * now, 127, 1),
                pltpu.roll(down * now, 1, 1),
            )

        before, here = tile_of(TILES - 1), tile_of(0)
        for tile in range(TILES):
            after = tile_of(tile + 1)
            at = slice(tile * 128, tile * 128 + 128)
            now = here[0]
            lati = wind_lat[level, :, at]
            up, down = jnp.maximum(lati, 0.0), jnp.minimum(lati, 0.0)
            from_east = jnp.where(lane == 127, after[2], here[2])
            from_west = jnp.where(lane == 0, before[3], here[3])
            from_north = jnp.where(
                lat == 7, rims.halo_north[index, tile : tile + 1, :], pltpu.roll(up * now, 7, 0)
            )
            from_south = jnp.where(
                lat == 0, rims.halo_south[index, tile : tile + 1, :], pltpu.roll(down * now, 1, 0)
            )
            new = (
                (here[1] - up + down) * now
                + from_east
                - from_west
                + from_north
                - from_south
                + forcing[(NT - 1 - step) * LEVELS + level, tile]
            )
            adjoint[index + LEVELS, tile] = new

            rims.edge_south[index + LEVELS, tile : tile + 1, :] = (up * new)[0:1, :]
            rims.edge_north[index + LEVELS, tile : tile + 1, :] = (down * new)[7:8, :]
            before, here = here, after

        @pl.when(index < (NT - 1) * LEVELS)
        def _():
            rims.start(index + LEVELS)

        return carry

    lax.fori_loop(0, NT * LEVELS, retreat, 0)

    for_peers(group, lambda peer: field_copy(peer, group).start())
    for level in range(LEVELS):
        column[LEVELS * group + level] = adjoint[NT * LEVELS + level, group]

    for_peers(group, lambda peer: dep_copy(group, peer).wait_recv())
    hit = lax.broadcasted_iota(I32, (GROUPS, 1024), 0) == dest[...]
    hit = jnp.where(hit, 1.0, 0.0).astype(BF16)
    spread_out = None
    for part in split_three(returned[:, 0, :]):
        term = lax.dot_general(
            part, hit, (((0,), (0,)), ((), ())), preferred_element_type=F32
        )
        spread_out = term if spread_out is None else spread_out + term
    place = lax.broadcasted_iota(I32, (128, 1024), 0)
    departure[...] = jnp.sum(
        jnp.where(place == slots[...], spread_out, 0.0), axis=0, keepdims=True
    )

    for load in loads:
        load.wait()
    root = vert_root[...].T
    for_peers(group, lambda peer: field_copy(group, peer).wait_recv())
    for lat_row in range(8):
        weighted = spread[:, lat_row, :] * column[:, lat_row, :]
        mixed = jnp.dot(
            root, weighted, precision=lax.Precision.HIGHEST, preferred_element_type=F32
        )
        gradient[:, lat_row, :] = control[:, lat_row, :] + mixed
    for_peers(group, lambda peer: field_copy(peer, group).wait_send())
    for_peers(group, lambda peer: dep_copy(peer, group).wait_send())
    rims.drain()


def per_device(
    control, spread, vert_root, wind_lon, wind_lat,
    obs_dest, obs_cells, obs_time, obs_value, obs_weight, obs_rinv,
):
    count = obs_time.shape[0]
    dest = obs_dest.reshape(1, count)
    fields = (NT + 1) * LEVELS
    wide, long = control.shape, (LEVELS, 8, TILES * 128)
    states, received, rows, slots, lon, lat, owner = pl.pallas_call(
        forward_kernel,
        out_shape=(
            jax.ShapeDtypeStruct((fields, TILES, 8, 128), F32),
            jax.ShapeDtypeStruct((GROUPS, 8, 128), F32),
            jax.ShapeDtypeStruct((GROUPS * 8, 128), I32),
            jax.ShapeDtypeStruct((1, count), I32),
            jax.ShapeDtypeStruct(long, F32),
            jax.ShapeDtypeStruct(long, F32),
            jax.ShapeDtypeStruct((1, count), I32),
        ),
        in_specs=[in_hbm()] * 11,
        out_specs=(in_vmem(),) * 7,
        scratch_shapes=[
            pltpu.VMEM(wide, F32),
            pltpu.VMEM(wide, F32),
            pltpu.VMEM((128, 128), F32),
            pltpu.VMEM((4, count), I32),
            pltpu.VMEM((1, count), I32),
            pltpu.VMEM((1, count), F32),
            pltpu.VMEM((4, count), F32),
            pltpu.VMEM((1, count), F32),
            pltpu.SemaphoreType.DMA((11,)),
            pltpu.VMEM(wide, F32),
            pltpu.VMEM((GROUPS, 8, 128), F32),
        ]
        + [pltpu.SemaphoreType.DMA((GROUPS,))] * 4
        + Rims.scratch(),
        compiler_params=pltpu.CompilerParams(
            collective_id=0, has_side_effects=True, vmem_limit_bytes=48 << 20
        ),
        name="forward",
    )(
        *map(stay, (
            control, spread, vert_root, wind_lon, wind_lat, dest, obs_cells,
            obs_time.reshape(1, count), obs_value.reshape(1, count), obs_weight,
            obs_rinv.reshape(1, count),
        ))
    )
    forcing, owner_dep = pl.pallas_call(
        obs_kernel,
        out_shape=(
            jax.ShapeDtypeStruct((fields * ROWS, 128), F32),
            jax.ShapeDtypeStruct((GROUPS, 1, 128), F32),
        ),
        in_specs=[in_vmem()] * 3,
        out_specs=(in_vmem(),) * 2,
        scratch_shapes=[
            pltpu.VMEM((4 * CAP, 128), F32),
            pltpu.VMEM((8 * CAP, 128), F32),
            pltpu.SMEM((4, 8, 128), I32),
            pltpu.SemaphoreType.DMA((4,)),
        ]
        + [pltpu.VMEM((fields * ROWS, 128), F32)] * ACCS,
        compiler_params=pltpu.CompilerParams(vmem_limit_bytes=48 << 20),
        name="observe",
    )(rows, received, states.reshape(fields * ROWS, 128))
    gradient, departure = pl.pallas_call(
        adjoint_kernel,
        out_shape=(
            jax.ShapeDtypeStruct(control.shape, F32),
            jax.ShapeDtypeStruct((1, count), F32),
        ),
        in_specs=[in_hbm()] * 3 + [in_vmem()] * 6,
        out_specs=(in_vmem(),) * 2,
        scratch_shapes=[
            pltpu.VMEM(wide, F32),
            pltpu.VMEM(wide, F32),
            pltpu.VMEM((128, 128), F32),
            pltpu.SemaphoreType.DMA((3,)),
            pltpu.VMEM((fields, TILES, 8, 128), F32),
            pltpu.VMEM((128, 8, 128), F32),
            pltpu.VMEM((GROUPS, 1, 128), F32),
        ]
        + [pltpu.SemaphoreType.DMA((GROUPS,))] * 4
        + Rims.scratch(),
        compiler_params=pltpu.CompilerParams(
            collective_id=1, has_side_effects=True, vmem_limit_bytes=48 << 20
        ),
        name="retreat",
    )(
        stay(control), stay(spread), stay(vert_root), lon, lat,
        forcing.reshape(fields, TILES, 8, 128), owner_dep, owner, slots,
    )
    return gradient, departure.reshape(count)


def solution(mesh):
    in_specs = (
        P(None, "obs", "horiz"),
        P(None, "obs", "horiz"),
        P(),
        P("horiz", "obs", None),
        P("horiz", "obs", None),
        P(("obs", "horiz"), None),
        P(None, ("obs", "horiz")),
        P(("obs", "horiz")),
        P(("obs", "horiz")),
        P(None, ("obs", "horiz")),
        P(("obs", "horiz")),
    )
    out_specs = (P(None, "obs", "horiz"), P(("obs", "horiz")))
    return jax.shard_map(
        per_device, mesh=mesh, in_specs=in_specs, out_specs=out_specs, check_vma=False
    )
```
